32 devices in a mesh: groups: 2 (over y), adapter: 4 (over x, core), mp: 4 (over z).
Axes of the slice: x: 2, y: 2, z: 4, core: 2. Of those that a mesh axis runs over, the one named last changes fastest.
Arguments:
- hidden: bfloat16 [3072, 16384], P(('groups', 'adapter'), 'mp'), parts along dimension 0, may hold values from -6 to 6
- adapter_ids: int32 [3072], P(('groups', 'adapter')), parts along dimension 0, may hold values from 0 to 7, as said below
- down_weight: bfloat16 [16384, 4096], P('mp'), may hold values from -0.0625 to 0.0625
- adapter_down: bfloat16 [16, 64, 16384], P(('groups', 'adapter'), None, 'mp'), parts along dimension 0, may hold values from -6 to 6
- adapter_up: bfloat16 [16, 64, 4096], P(('groups', 'adapter'), None, 'mp'), parts along dimension 0, may hold values from -6 to 6
- migration_plan: int32 [16], P(('groups', 'adapter')), parts along dimension 0, may hold values from 0 to 7, each once
Outputs:
- layer_result: bfloat16 [3072, 4096], P(('groups', 'adapter'), 'mp'), parts along dimension 0
- moved_down: bfloat16 [16, 64, 16384], P(('groups', 'adapter'), None, 'mp'), parts along dimension 0
- moved_up: bfloat16 [16, 64, 4096], P(('groups', 'adapter'), None, 'mp'), parts along dimension 0
The draws below stay inside these ranges and needn't reach their ends.
There are 2 independent parts, one for each index of `groups`. The reference program is written for one: setup_inputs(seed, part) draws one part's arguments, and reference() takes and returns one part's arrays. A program takes and returns all parts, laid end to end along the dimension named above; an argument that names none is the same for every part. Nothing has to cross between parts.
Inputs may be any that keep to these rules, and one draw needn't show every extreme that they name: `adapter_ids`: among the 384 requests of one index of adapter, at most 192 ask for one adapter; in every draw one adapter is asked for by exactly 192 requests of every index. `migration_plan`: each adapter appears exactly once.
All inputs are finite; a program needn't handle non-finite values.
Results may differ from the reference program's by a relative error of at most 0.012.
Values may be sent and summed in bfloat16 or wider, within the bound.
A program may use at most 128 MiB of HBM per device.

```python
import math
import jax
import jax.numpy as jnp
from jax import lax

OUTPUT_WINDOW = 4096
FF = 16384
RANK = 64
ROWS_DEV = 384
ADAPTER_COUNT = 8
TOKENS = 1536
CAP = 192
BLOCKS = 4
UNITS = 4096
N_ADAPTER = 4


def draw_adapter_ids(key, part):
    block_count = TOKENS // ROWS_DEV
    slot_total = ADAPTER_COUNT * CAP
    hot_key, boost_key, blocks_key = jax.random.split(key, 3)
    hot_adapter = jax.random.randint(hot_key, (), 0, ADAPTER_COUNT)
    boosts = jax.random.randint(boost_key, (ADAPTER_COUNT,), 0, 4) * 512
    slot_owner = jnp.arange(slot_total, dtype=jnp.int32) // CAP

    def one_block(block_key):
        noise_key, order_key, shuffle_key = jax.random.split(block_key, 3)
        noise = jax.random.randint(noise_key, (slot_total,), 0, 1024)
        scores = noise + boosts[slot_owner]
        scores = jnp.where(slot_owner == hot_adapter, 4096, scores)
        breaker = jax.random.permutation(order_key, slot_total)
        distinct = scores * slot_total + breaker
        ranking = jnp.argsort(-distinct, stable=True)[:ROWS_DEV]
        chosen = slot_owner[ranking]
        return chosen[jax.random.permutation(shuffle_key, ROWS_DEV)]
    block_keys = jax.random.split(blocks_key, block_count)
    return jax.vmap(one_block)(block_keys).reshape(-1).astype(jnp.int32)


def raised(drawn, stream_key, source, target, parts, factor):
    owner, partner = [(jnp.arange(drawn.shape[axis_at]) // (drawn.shape[axis_at] // parts)).reshape([-1 if axis == axis_at else 1 for axis in range(drawn.ndim)]) for axis_at in (source, target)]
    chosen = jax.random.permutation(stream_key, parts)[partner]
    strong = (owner == chosen) | (owner == (partner + parts // 2) % parts)
    return jnp.where(strong, factor * drawn, drawn)


def levels(stream_key, extent, cuts, least, largest):
    def one(dim, blocks):
        steps = jax.random.uniform(jax.random.fold_in(jax.random.fold_in(stream_key, 6), dim), (blocks,), jnp.float32, least / len(cuts), largest / len(cuts))
        return jnp.repeat(jnp.exp(steps), extent[dim] // blocks).reshape((-1,) + (1,) * (len(extent) - dim - 1))

    level = one(*cuts[0])
    for cut in cuts[1:]:
        level = level * one(*cut)
    return level


def scatter_about(stream_key, dims, scale, bound, cuts=(), kind=jnp.bfloat16):
    loudness = levels(stream_key, dims, cuts, -0.22, 0.18) if cuts else 1.0
    drawn = jax.random.normal(stream_key, dims, jnp.float32) * scale * loudness
    return jnp.minimum(jnp.maximum(drawn, -bound), bound).astype(kind)


def noise_with(stream_key, extent, scale, reach, pieces, heavy, held_as=jnp.bfloat16):
    values = scale * jax.random.normal(stream_key, extent, jnp.float32)
    if pieces:
        values = values * levels(stream_key, extent, pieces, -0.22, 0.18)
    return jnp.clip(raised(values, jax.random.fold_in(stream_key, 3), *heavy), -reach, reach).astype(held_as)


def setup_inputs(seed: int = 0, part: int = 0) -> dict:
    splits = jax.random.split(jax.random.key(seed), 7)
    part_splits = jax.random.split(jax.random.fold_in(splits[6], part), 7)
    return {
        "hidden": scatter_about(part_splits[0], (TOKENS, FF), 1.0, 6.0, ((0, 4), (1, 4))),
        "adapter_ids": draw_adapter_ids(jax.random.fold_in(jax.random.fold_in(splits[6], part), 71), part),
        "down_weight": noise_with(splits[2], (FF, OUTPUT_WINDOW), FF ** -0.5, 0.0625, ((0, 4),), (0, 1, 4, 2.0)),
        "adapter_down": scatter_about(part_splits[3], (ADAPTER_COUNT, RANK, FF), 1.0, 6.0, ((0, 4), (2, 4))),
        "adapter_up": scatter_about(part_splits[4], (ADAPTER_COUNT, RANK, OUTPUT_WINDOW), 1.0, 6.0, ((0, 4), (2, 4))),
        "migration_plan": jax.random.permutation(part_splits[5], ADAPTER_COUNT).astype(jnp.int32),
    }


def reference(hidden, adapter_ids, down_weight, adapter_down, adapter_up, migration_plan):

    def add_block(running, block):
        columns = lax.dynamic_slice_in_dim(hidden, block * UNITS, UNITS, 1)
        weights = lax.dynamic_slice_in_dim(down_weight, block * UNITS, UNITS, 0)
        product = jnp.dot(columns, weights, preferred_element_type=jnp.float32)
        rounded = lax.optimization_barrier(product.astype(jnp.bfloat16))
        return (running + rounded.astype(jnp.float32), None)
    base_product, ignored = lax.scan(add_block, jnp.zeros((TOKENS, OUTPUT_WINDOW), jnp.float32), jnp.arange(BLOCKS, dtype=jnp.int32))
    slot_space = CAP * N_ADAPTER
    catalog = jnp.arange(ADAPTER_COUNT, dtype=jnp.int32)
    matches = adapter_ids[:, None] == catalog[None, :]
    counted = (jnp.cumsum(matches.astype(jnp.int32), axis=0) - 1).astype(jnp.int32)
    ranking = lax.optimization_barrier(jnp.sum(jnp.where(matches, counted, 0), axis=1)).astype(jnp.int32)
    slot_position = (adapter_ids * slot_space + ranking).astype(jnp.int32)
    row_of_slot = jnp.zeros((ADAPTER_COUNT * slot_space,), jnp.int32).at[slot_position].set(jnp.arange(TOKENS, dtype=jnp.int32))

    def one_adapter(packed):
        row_list, down_matrix, up_matrix = packed
        taken = hidden[row_list]
        factor = lax.dot_general(taken, down_matrix, (((1,), (1,)), ((), ())), preferred_element_type=jnp.float32)
        factor = (factor * (1.0 / math.sqrt(FF))).astype(jnp.bfloat16)
        update = jnp.dot(factor, up_matrix, preferred_element_type=jnp.float32)
        return (update * (0.5 / math.sqrt(RANK))).astype(jnp.bfloat16)
    update_rows = lax.map(one_adapter, (row_of_slot.reshape(ADAPTER_COUNT, slot_space), adapter_down, adapter_up))
    low_rank_change = update_rows.reshape(ADAPTER_COUNT * slot_space, OUTPUT_WINDOW)[slot_position]
    layer_result = (base_product + low_rank_change.astype(jnp.float32)).astype(jnp.bfloat16)
    return (layer_result, adapter_down[migration_plan], adapter_up[migration_plan])
```

```python
import functools
import math

import jax
import jax.numpy as jnp
from jax import lax
from jax.experimental import pallas as pl
from jax.experimental.pallas import tpu as pltpu
from jax.sharding import PartitionSpec as P

MESH = pl.DeviceIdType.MESH
SLOTS = 3
STRIDE = 3


def kernel(
    n, na, tile, inv_units, out_scale,
    plan_ref, hidden_ref, ids_ref, down_ref, up_ref, weight_ref,
    out_ref, mdown_ref, mup_ref,
    weights, prod, recv, store_down, store_up, fac, lora, spread, total,
    w_sem, z_send, z_recv, local_sem, x_send, x_recv, f_send, f_recv,
):
    me = lax.axis_index("mp")
    ad = lax.axis_index("adapter")
    rows = hidden_ref.shape[0]
    width = out_ref.shape[1]
    tiles = width // tile
    count = n * tiles
    local_count, rank, _ = mdown_ref.shape
    before, after = me, n - 1 - me
    far, near = jnp.maximum(before, after), jnp.minimum(before, after)
    lone = far - near
    right_far = (after > before).astype(jnp.int32)

    def visit(s):
        t = jnp.maximum(s - lone, 0)
        k = jnp.where(s < lone, far - s, near - t // 2)
        on_far = jnp.where(s < lone, 1, t % 2)
        right = jnp.where(on_far == 1, right_far, 1 - right_far)
        return me + jnp.where(right == 1, k, -k), right

    def weight_copy(t, slot):
        d, _ = visit(t // tiles)
        col = pl.multiple_of(d * width + (t % tiles) * tile, tile)
        return pltpu.make_async_copy(
            weight_ref.at[:, pl.ds(col, tile)], weights.at[slot], w_sem.at[slot]
        )

    for t in range(SLOTS - 1):
        weight_copy(t, t).start()
    own_down = pltpu.make_async_copy(down_ref, store_down.at[ad], local_sem.at[0])
    own_up = pltpu.make_async_copy(up_ref, store_up.at[ad], local_sem.at[1])
    own_down.start()
    own_up.start()

    bits = []
    bit = na // 2
    while bit:
        bits.append(bit)
        bit //= 2

    def partner(b):
        return ad + jnp.where((ad // b) % 2 == 1, -b, b)

    def slot_of(s):
        x = ad
        for b in bits:
            if s & b:
                x = x + jnp.where((ad // b) % 2 == 1, -b, b)
        return x

    barrier = pltpu.get_barrier_semaphore()

    @pl.loop(1, n)
    def _(i):
        pl.semaphore_signal(
            barrier, inc=1, device_id={"mp": (me + i) % n}, device_id_type=MESH
        )

    for b in bits:
        pl.semaphore_signal(
            barrier, inc=1, device_id={"adapter": partner(b)}, device_id_type=MESH
        )
    pl.semaphore_wait(barrier, n - 1 + len(bits))

    def adapter_copies(b, s):
        slot = slot_of(s)
        out = []
        for i, (mine, store) in enumerate(((down_ref, store_down), (up_ref, store_up))):
            out.append(
                pltpu.make_async_remote_copy(
                    src_ref=mine if s == 0 else store.at[slot],
                    dst_ref=store.at[slot],
                    send_sem=x_send.at[i, b ^ s],
                    recv_sem=x_recv.at[i, b ^ s],
                    device_id={"adapter": partner(b)},
                    device_id_type=MESH,
                )
            )
        return out

    for b in bits:
        for c in adapter_copies(b, 0):
            c.start()

    def block_copy(d, right, j):
        return pltpu.make_async_remote_copy(
            src_ref=prod.at[d, j],
            dst_ref=recv.at[right, d, j],
            send_sem=z_send.at[d, j],
            recv_sem=z_recv.at[right, d, j],
            device_id={"mp": jnp.where(right == 1, (me + 1) % n, (me + n - 1) % n)},
            device_id_type=MESH,
        )

    def first_in_line(right):
        return jnp.where(right == 1, before, after) == 0

    def forward(item):
        d, right = visit(item // tiles)
        j = item % tiles

        @pl.when(jnp.logical_not(first_in_line(right)))
        def _():
            copy = block_copy(d, right, j)
            copy.wait_recv()
            prod[d, j] = (
                prod[d, j].astype(jnp.float32) + recv[right, d, j].astype(jnp.float32)
            ).astype(jnp.bfloat16)
            copy.start()

    start_forward = tiles + 1
    early = max(0, min(-(-(count - start_forward) // STRIDE), (n - 2) * tiles))

    @pl.loop(0, count)
    def _(t):
        slot = t % SLOTS

        @pl.when(t + SLOTS - 1 < count)
        def _():
            weight_copy(t + SLOTS - 1, (t + SLOTS - 1) % SLOTS).start()

        weight_copy(t, slot).wait()
        d, right = visit(t // tiles)
        j = t % tiles
        prod[d, j] = jnp.dot(
            hidden_ref[...], weights[slot], preferred_element_type=jnp.float32
        ).astype(jnp.bfloat16)

        @pl.when(jnp.logical_and(d != me, first_in_line(right)))
        def _():
            block_copy(d, right, j).start()

        if early:
            step = t - start_forward

            @pl.when((step >= 0) & (step % STRIDE == 0) & (step < early * STRIDE))
            def _():
                forward(jnp.maximum(step, 0) // STRIDE)

    @pl.loop(early, (n - 2) * tiles)
    def _(i):
        forward(i)

    held = [0]
    for b in bits:
        for s in held:
            if s:
                for c in adapter_copies(b, s):
                    c.start()
        if b == bits[-1]:

            @pl.loop((n - 2) * tiles, (n - 1) * tiles)
            def _(i):
                forward(i)

        for s in held:
            for c in adapter_copies(b, s):
                c.wait_recv()
        held = held + [s ^ b for s in held]

    own_down.wait()
    own_up.wait()

    total_adapters = na * local_count
    stacked = store_down[...].reshape(total_adapters * rank, store_down.shape[2])
    every = lax.dot_general(
        stacked, hidden_ref[...], (((1,), (1,)), ((), ())), preferred_element_type=jnp.float32
    )
    ids = ids_ref[...]
    part = jnp.zeros((rank, rows), jnp.float32)
    for g in range(total_adapters):
        part = part + jnp.where(ids == g, every[g * rank : (g + 1) * rank], 0.0)
    fac[me] = part.astype(jnp.bfloat16)

    def factor_copy(source, target):
        return pltpu.make_async_remote_copy(
            src_ref=fac.at[source],
            dst_ref=fac.at[source],
            send_sem=f_send.at[target],
            recv_sem=f_recv.at[source],
            device_id={"mp": target},
            device_id_type=MESH,
        )

    @pl.loop(1, n)
    def _(i):
        factor_copy(me, (me + i) % n).start()

    for s in range(local_count):
        g = plan_ref[s]
        mdown_ref[s] = store_down[g // local_count, pl.ds((g % local_count) * rank, rank), :]
        mup_ref[s] = store_up[g // local_count, pl.ds((g % local_count) * rank, rank), :]

    @pl.loop(1, n)
    def _(i):
        other = (me + i) % n
        factor_copy(other, other).wait_recv()

    factor = fac[0].astype(jnp.float32)
    for i in range(1, n):
        factor = factor + fac[i].astype(jnp.float32)
    factor = (factor * inv_units).astype(jnp.bfloat16).astype(jnp.float32)
    for g in range(total_adapters):
        spread[g * rank : (g + 1) * rank, :] = jnp.where(ids == g, factor, 0.0).astype(
            jnp.bfloat16
        )
    turned = jnp.transpose(spread[...].astype(jnp.float32)).astype(jnp.bfloat16)
    for j in range(tiles):
        cols = slice(j * tile, (j + 1) * tile)
        lora[:, cols] = (
            jnp.dot(
                turned,
                store_up[:, :, cols].reshape(total_adapters * rank, tile),
                preferred_element_type=jnp.float32,
            )
            * out_scale
        ).astype(jnp.bfloat16)

    for j in range(tiles):
        cols = slice(j * tile, (j + 1) * tile)
        total[...] = prod[me, j].astype(jnp.float32)
        for right, there in ((1, before > 0), (0, after > 0)):

            @pl.when(there)
            def _(right=right, j=j):
                block_copy(me, jnp.int32(right), j).wait_recv()
                total[...] += recv[right, me, j].astype(jnp.float32)

        out_ref[:, cols] = (total[...] + lora[:, cols].astype(jnp.float32)).astype(jnp.bfloat16)

    @pl.loop(0, (n - 1) * tiles)
    def _(i):
        d, right = visit(i // tiles)
        block_copy(d, right, i % tiles).wait_send()

    @pl.loop(1, n)
    def _(i):
        factor_copy(me, (me + i) % n).wait_send()

    held = [0]
    for b in bits:
        for s in held:
            for c in adapter_copies(b, s):
                c.wait_send()
        held = held + [s ^ b for s in held]


def per_device(n, na, hidden, adapter_ids, down_weight, adapter_down, adapter_up, migration_plan):
    rows, units = hidden.shape
    local_count, rank, width = adapter_up.shape
    tile = min(256, width)
    tiles = width // tile
    stack = local_count * rank
    vmem = pl.BlockSpec(memory_space=pltpu.VMEM)
    bf16 = jnp.bfloat16
    result, moved_down, moved_up = pl.pallas_call(
        functools.partial(
            kernel, n, na, tile, 1.0 / math.sqrt(units * n), 0.5 / math.sqrt(rank)
        ),
        out_shape=(
            jax.ShapeDtypeStruct((rows, width), bf16),
            jax.ShapeDtypeStruct(adapter_down.shape, bf16),
            jax.ShapeDtypeStruct(adapter_up.shape, bf16),
        ),
        in_specs=[pl.BlockSpec(memory_space=pltpu.SMEM), vmem, vmem, vmem, vmem]
        + [pl.BlockSpec(memory_space=pl.ANY)],
        out_specs=(vmem, vmem, vmem),
        scratch_shapes=[
            pltpu.VMEM((SLOTS, units, tile), bf16),
            pltpu.VMEM((n, tiles, rows, tile), bf16),
            pltpu.VMEM((2, n, tiles, rows, tile), bf16),
            pltpu.VMEM((na, stack, units), bf16),
            pltpu.VMEM((na, stack, width), bf16),
            pltpu.VMEM((n, rank, rows), bf16),
            pltpu.VMEM((rows, width), bf16),
            pltpu.VMEM((na * stack, rows), bf16),
            pltpu.VMEM((rows, tile), jnp.float32),
            pltpu.SemaphoreType.DMA((SLOTS,)),
            pltpu.SemaphoreType.DMA((n, tiles)),
            pltpu.SemaphoreType.DMA((2, n, tiles)),
            pltpu.SemaphoreType.DMA((2,)),
            pltpu.SemaphoreType.DMA((2, na)),
            pltpu.SemaphoreType.DMA((2, na)),
            pltpu.SemaphoreType.DMA((n,)),
            pltpu.SemaphoreType.DMA((n,)),
        ],
        compiler_params=pltpu.CompilerParams(
            collective_id=0, has_side_effects=True, vmem_limit_bytes=56 << 20
        ),
    )(
        migration_plan,
        hidden,
        adapter_ids[None, :],
        adapter_down.reshape(stack, units),
        adapter_up.reshape(stack, width),
        down_weight,
    )
    return result, moved_down, moved_up


def solution(mesh):
    placed = (
        P(("groups", "adapter"), "mp"),
        P(("groups", "adapter")),
        P("mp", None),
        P(("groups", "adapter"), None, "mp"),
        P(("groups", "adapter"), None, "mp"),
        P(("groups", "adapter")),
    )
    return jax.shard_map(
        functools.partial(per_device, mesh.shape["mp"], mesh.shape["adapter"]),
        mesh=mesh,
        in_specs=placed,
        out_specs=(
            P(("groups", "adapter"), "mp"),
            P(("groups", "adapter"), None, "mp"),
            P(("groups", "adapter"), None, "mp"),
        ),
        check_vma=False,
    )
```

```python
import functools
import math

import jax
import jax.numpy as jnp
from jax import lax
from jax.experimental import pallas as pl
from jax.experimental.pallas import tpu as pltpu
from jax.sharding import PartitionSpec as P

MESH = pl.DeviceIdType.MESH
SLOTS = 3
STRIDE = 3


def kernel(
    n, na, tile, inv_units, out_scale,
    plan_ref, ids_ref, hidden_hbm, down_ref, up_ref, weight_ref,
    out_ref, mdown_ref, mup_ref,
    weights, hidden_ref, prod, recv, store_down, store_up, fac, fac_in, fac_sum, lora, spread, total,
    w_sem, z_send, z_recv, local_sem, x_send, x_recv, f_send, f_recv,
):
    me = lax.axis_index("mp")
    ad = lax.axis_index("adapter")
    rows = hidden_ref.shape[0]
    width = out_ref.shape[1]
    tiles = width // tile
    count = n * tiles
    local_count, rank, _ = mdown_ref.shape
    before, after = me, n - 1 - me
    far, near = jnp.maximum(before, after), jnp.minimum(before, after)
    lone = far - near
    right_far = (after > before).astype(jnp.int32)

    def visit(s):
        t = jnp.maximum(s - lone, 0)
        k = jnp.where(s < lone, far - s, near - t // 2)
        on_far = jnp.where(s < lone, 1, t % 2)
        right = jnp.where(on_far == 1, right_far, 1 - right_far)
        return me + jnp.where(right == 1, k, -k), right

    def weight_copy(t, slot):
        d, _ = visit(t // tiles)
        col = pl.multiple_of(d * width + (t % tiles) * tile, tile)
        return pltpu.make_async_copy(
            weight_ref.at[:, pl.ds(col, tile)], weights.at[slot], w_sem.at[slot]
        )

    own_hidden = pltpu.make_async_copy(hidden_hbm, hidden_ref, local_sem.at[2])
    own_hidden.start()
    for t in range(SLOTS - 1):
        weight_copy(t, t).start()
    own_down = pltpu.make_async_copy(down_ref, store_down.at[ad], local_sem.at[0])
    own_up = pltpu.make_async_copy(up_ref, store_up.at[ad], local_sem.at[1])

    bits = []
    bit = na // 2
    while bit:
        bits.append(bit)
        bit //= 2

    def partner(b):
        return ad + jnp.where((ad // b) % 2 == 1, -b, b)

    def slot_of(s):
        x = ad
        for b in bits:
            if s & b:
                x = x + jnp.where((ad // b) % 2 == 1, -b, b)
        return x

    barrier = pltpu.get_barrier_semaphore()

    for here, step in ((before > 0, n - 1), (after > 0, 1)):

        @pl.when(here)
        def _(step=step):
            pl.semaphore_signal(
                barrier, inc=1, device_id={"mp": (me + step) % n}, device_id_type=MESH
            )

    for b in bits:
        pl.semaphore_signal(
            barrier, inc=1, device_id={"adapter": partner(b)}, device_id_type=MESH
        )
    pl.semaphore_wait(
        barrier, (before > 0).astype(jnp.int32) + (after > 0).astype(jnp.int32) + len(bits)
    )

    def adapter_copy(i, b, s):
        slot = slot_of(s)
        mine, store = ((down_ref, store_down), (up_ref, store_up))[i]
        return pltpu.make_async_remote_copy(
            src_ref=mine if s == 0 else store.at[slot],
            dst_ref=store.at[slot],
            send_sem=x_send.at[i, b ^ s],
            recv_sem=x_recv.at[i, b ^ s],
            device_id={"adapter": partner(b)},
            device_id_type=MESH,
        )

    for b in bits:
        adapter_copy(0, b, 0).start()
    own_down.start()
    own_up.start()
    own_hidden.wait()

    def block_copy(d, right, j):
        return pltpu.make_async_remote_copy(
            src_ref=prod.at[d, j],
            dst_ref=recv.at[right, d, j],
            send_sem=z_send.at[d, j],
            recv_sem=z_recv.at[right, d, j],
            device_id={"mp": jnp.where(right == 1, (me + 1) % n, (me + n - 1) % n)},
            device_id_type=MESH,
        )

    def first_in_line(right):
        return jnp.where(right == 1, before, after) == 0

    def forward(item):
        d, right = visit(item // tiles)
        j = item % tiles

        @pl.when(jnp.logical_not(first_in_line(right)))
        def _():
            copy = block_copy(d, right, j)
            copy.wait_recv()
            prod[d, j] = (
                prod[d, j].astype(jnp.float32) + recv[right, d, j].astype(jnp.float32)
            ).astype(jnp.bfloat16)
            copy.start()

    queued = (n - 1) * tiles - 3 * tiles // 4
    start_forward = tiles + 1
    early = max(0, min(-(-(count - start_forward) // STRIDE), (n - 2) * tiles))

    @pl.loop(0, count)
    def _(t):
        slot = t % SLOTS

        @pl.when(t + SLOTS - 1 < count)
        def _():
            weight_copy(t + SLOTS - 1, (t + SLOTS - 1) % SLOTS).start()

        weight_copy(t, slot).wait()
        d, right = visit(t // tiles)
        j = t % tiles
        prod[d, j] = jnp.dot(
            hidden_ref[...], weights[slot], preferred_element_type=jnp.float32
        ).astype(jnp.bfloat16)

        @pl.when((t < queued) & first_in_line(right))
        def _():
            block_copy(d, right, j).start()

        if early:
            step = t - start_forward

            @pl.when((step >= 0) & (step % STRIDE == 0) & (step < early * STRIDE))
            def _():
                forward(jnp.maximum(step, 0) // STRIDE)

    @pl.loop(early, (n - 2) * tiles)
    def _(i):
        forward(i)

    def relay(i, before_last):
        held = [0]
        for b in bits:
            for s in held:
                if s:
                    adapter_copy(i, b, s).start()
            if b == bits[-1]:
                before_last()
            for s in held:
                adapter_copy(i, b, s).wait_recv()
            held = held + [s ^ b for s in held]

    def rest():
        for b in bits:
            adapter_copy(1, b, 0).start()

        @pl.loop((n - 2) * tiles, (n - 1) * tiles)
        def _(i):
            forward(i)

    relay(0, rest)
    own_down.wait()

    total_adapters = na * local_count
    stacked = store_down[...].reshape(total_adapters * rank, store_down.shape[2])
    every = lax.dot_general(
        stacked, hidden_ref[...], (((1,), (1,)), ((), ())), preferred_element_type=jnp.float32
    )
    ids = ids_ref[...].reshape(1, rows)
    part = jnp.zeros((rank, rows), jnp.float32)
    for g in range(total_adapters):
        part = part + jnp.where(ids == g, every[g * rank : (g + 1) * rank], 0.0)

    def factor_copy(right):
        return pltpu.make_async_remote_copy(
            src_ref=fac.at[right],
            dst_ref=fac_in.at[right],
            send_sem=f_send.at[right],
            recv_sem=f_recv.at[right],
            device_id={"mp": (me + 1) % n if right else (me + n - 1) % n},
            device_id_type=MESH,
        )

    mine = part.astype(jnp.bfloat16)
    fac[0] = mine
    fac[1] = mine
    ends = ((1, before, after), (0, after, before))
    for right, upstream, _ in ends:

        @pl.when(upstream == 0)
        def _(right=right):
            factor_copy(right).start()

    @pl.loop(queued, (n - 1) * tiles)
    def _(i):
        d, right = visit(i // tiles)

        @pl.when(first_in_line(right))
        def _():
            block_copy(d, right, i % tiles).start()

    relay(1, lambda: None)
    own_up.wait()
    for s in range(local_count):
        g = plan_ref[s]
        mdown_ref[s] = store_down[g // local_count, pl.ds((g % local_count) * rank, rank), :]
        mup_ref[s] = store_up[g // local_count, pl.ds((g % local_count) * rank, rank), :]

    fac_sum[...] = part
    for right, upstream, downstream in ends:

        @pl.when(upstream > 0)
        def _(right=right, downstream=downstream):
            factor_copy(right).wait_recv()
            came = fac_in[right].astype(jnp.float32)
            fac_sum[...] += came

            @pl.when(downstream > 0)
            def _():
                fac[right] = (fac[right].astype(jnp.float32) + came).astype(jnp.bfloat16)
                factor_copy(right).start()

    factor = fac_sum[...]
    factor = (factor * inv_units).astype(jnp.bfloat16).astype(jnp.float32)
    for g in range(total_adapters):
        spread[g * rank : (g + 1) * rank, :] = jnp.where(ids == g, factor, 0.0).astype(
            jnp.bfloat16
        )
    turned = jnp.transpose(spread[...].astype(jnp.float32)).astype(jnp.bfloat16)
    for j in range(tiles):
        cols = slice(j * tile, (j + 1) * tile)
        lora[:, cols] = (
            jnp.dot(
                turned,
                store_up[:, :, cols].reshape(total_adapters * rank, tile),
                preferred_element_type=jnp.float32,
            )
            * out_scale
        ).astype(jnp.bfloat16)

    for j in range(tiles):
        cols = slice(j * tile, (j + 1) * tile)
        total[...] = prod[me, j].astype(jnp.float32)
        for right, there in ((1, before > 0), (0, after > 0)):

            @pl.when(there)
            def _(right=right, j=j):
                block_copy(me, jnp.int32(right), j).wait_recv()
                total[...] += recv[right, me, j].astype(jnp.float32)

        out_ref[:, cols] = (total[...] + lora[:, cols].astype(jnp.float32)).astype(jnp.bfloat16)

    @pl.loop(0, (n - 1) * tiles)
    def _(i):
        d, right = visit(i // tiles)
        block_copy(d, right, i % tiles).wait_send()

    for right, _, downstream in ends:

        @pl.when(downstream > 0)
        def _(right=right):
            factor_copy(right).wait_send()

    held = [0]
    for b in bits:
        for s in held:
            for i in range(2):
                adapter_copy(i, b, s).wait_send()
        held = held + [s ^ b for s in held]


def place(*refs):
    sources, targets, sems = refs[:3], refs[3:6], refs[6]
    copies = [pltpu.make_async_copy(a, b, sems.at[i]) for i, (a, b) in enumerate(zip(sources, targets))]
    for c in copies:
        c.start()
    for c in copies:
        c.wait()


def per_device(n, na, hidden, adapter_ids, down_weight, adapter_down, adapter_up, migration_plan):
    rows, units = hidden.shape
    local_count, rank, width = adapter_up.shape
    tile = min(256, width)
    tiles = width // tile
    stack = local_count * rank
    vmem = pl.BlockSpec(memory_space=pltpu.VMEM)
    anywhere = pl.BlockSpec(memory_space=pl.ANY)
    bf16 = jnp.bfloat16
    shapes = (
        jax.ShapeDtypeStruct((rows, width), bf16),
        jax.ShapeDtypeStruct(adapter_down.shape, bf16),
        jax.ShapeDtypeStruct(adapter_up.shape, bf16),
    )
    held = pl.pallas_call(
        functools.partial(
            kernel, n, na, tile, 1.0 / math.sqrt(units * n), 0.5 / math.sqrt(rank)
        ),
        out_shape=tuple(pltpu.VMEM(x.shape, x.dtype) for x in shapes),
        in_specs=[pl.BlockSpec(memory_space=pltpu.SMEM), vmem] + [anywhere] * 4,
        out_specs=(vmem, vmem, vmem),
        scratch_shapes=[
            pltpu.VMEM((SLOTS, units, tile), bf16),
            pltpu.VMEM((rows, units), bf16),
            pltpu.VMEM((n, tiles, rows, tile), bf16),
            pltpu.VMEM((2, n, tiles, rows, tile), bf16),
            pltpu.VMEM((na, stack, units), bf16),
            pltpu.VMEM((na, stack, width), bf16),
            pltpu.VMEM((2, rank, rows), bf16),
            pltpu.VMEM((2, rank, rows), bf16),
            pltpu.VMEM((rank, rows), jnp.float32),
            pltpu.VMEM((rows, width), bf16),
            pltpu.VMEM((na * stack, rows), bf16),
            pltpu.VMEM((rows, tile), jnp.float32),
            pltpu.SemaphoreType.DMA((SLOTS,)),
            pltpu.SemaphoreType.DMA((n, tiles)),
            pltpu.SemaphoreType.DMA((2, n, tiles)),
            pltpu.SemaphoreType.DMA((3,)),
            pltpu.SemaphoreType.DMA((2, na)),
            pltpu.SemaphoreType.DMA((2, na)),
            pltpu.SemaphoreType.DMA((2,)),
            pltpu.SemaphoreType.DMA((2,)),
        ],
        compiler_params=pltpu.CompilerParams(
            collective_id=0, has_side_effects=True, vmem_limit_bytes=56 << 20
        ),
    )(
        migration_plan,
        adapter_ids,
        hidden,
        adapter_down.reshape(stack, units),
        adapter_up.reshape(stack, width),
        down_weight,
    )
    return pl.pallas_call(
        place,
        out_shape=shapes,
        in_specs=[vmem] * 3,
        out_specs=(anywhere,) * 3,
        scratch_shapes=[pltpu.SemaphoreType.DMA((3,))],
    )(*(pltpu.with_memory_space_constraint(x, pltpu.VMEM) for x in held))


def solution(mesh):
    placed = (
        P(("groups", "adapter"), "mp"),
        P(("groups", "adapter")),
        P("mp", None),
        P(("groups", "adapter"), None, "mp"),
        P(("groups", "adapter"), None, "mp"),
        P(("groups", "adapter")),
    )
    return jax.shard_map(
        functools.partial(per_device, mesh.shape["mp"], mesh.shape["adapter"]),
        mesh=mesh,
        in_specs=placed,
        out_specs=(
            P(("groups", "adapter"), "mp"),
            P(("groups", "adapter"), None, "mp"),
            P(("groups", "adapter"), None, "mp"),
        ),
        check_vma=False,
    )
```

```python
import functools
import math

import jax
import jax.numpy as jnp
from jax import lax
from jax.experimental import pallas as pl
from jax.experimental.pallas import tpu as pltpu
from jax.sharding import PartitionSpec as P

MESH = pl.DeviceIdType.MESH
SLOTS = 3
STRIDE = 3


def kernel(
    n, na, tile, inv_units, out_scale,
    plan_ref, ids_ref, hidden_hbm, down_ref, up_ref, weight_ref,
    out_ref, mdown_ref, mup_ref,
    weights, hidden_ref, prod, recv, store_down, store_up, fac, fac_in, fac_sum, lora, spread, total,
    w_sem, z_send, z_recv, local_sem, x_send, x_recv, f_send, f_recv,
):
    me = lax.axis_index("mp")
    ad = lax.axis_index("adapter")
    rows = hidden_ref.shape[0]
    width = out_ref.shape[1]
    tiles = width // tile
    count = n * tiles
    local_count, rank, _ = mdown_ref.shape
    before, after = me, n - 1 - me
    far, near = jnp.maximum(before, after), jnp.minimum(before, after)
    lone = far - near
    right_far = (after > before).astype(jnp.int32)

    def visit(s):
        t = jnp.maximum(s - lone, 0)
        k = jnp.where(s < lone, far - s, near - t // 2)
        on_far = jnp.where(s < lone, 1, t % 2)
        right = jnp.where(on_far == 1, right_far, 1 - right_far)
        return me + jnp.where(right == 1, k, -k), right

    def weight_copy(t, slot):
        d, _ = visit(t // tiles)
        col = pl.multiple_of(d * width + (t % tiles) * tile, tile)
        return pltpu.make_async_copy(
            weight_ref.at[:, pl.ds(col, tile)], weights.at[slot], w_sem.at[slot]
        )

    own_hidden = pltpu.make_async_copy(hidden_hbm, hidden_ref, local_sem.at[2])
    own_hidden.start()
    for t in range(SLOTS - 1):
        weight_copy(t, t).start()
    own_down = pltpu.make_async_copy(down_ref, store_down.at[ad], local_sem.at[0])
    own_up = pltpu.make_async_copy(up_ref, store_up.at[ad], local_sem.at[1])

    bits = []
    bit = na // 2
    while bit:
        bits.append(bit)
        bit //= 2

    def partner(b):
        return ad + jnp.where((ad // b) % 2 == 1, -b, b)

    def slot_of(s):
        x = ad
        for b in bits:
            if s & b:
                x = x + jnp.where((ad // b) % 2 == 1, -b, b)
        return x

    barrier = pltpu.get_barrier_semaphore()

    for here, step in ((before > 0, n - 1), (after > 0, 1)):

        @pl.when(here)
        def _(step=step):
            pl.semaphore_signal(
                barrier, inc=1, device_id={"mp": (me + step) % n}, device_id_type=MESH
            )

    for b in bits:
        pl.semaphore_signal(
            barrier, inc=1, device_id={"adapter": partner(b)}, device_id_type=MESH
        )
    pl.semaphore_wait(
        barrier, (before > 0).astype(jnp.int32) + (after > 0).astype(jnp.int32) + len(bits)
    )

    def adapter_copy(i, b, s):
        slot = slot_of(s)
        mine, store = ((down_ref, store_down), (up_ref, store_up))[i]
        return pltpu.make_async_remote_copy(
            src_ref=mine if s == 0 else store.at[slot],
            dst_ref=store.at[slot],
            send_sem=x_send.at[i, b ^ s],
            recv_sem=x_recv.at[i, b ^ s],
            device_id={"adapter": partner(b)},
            device_id_type=MESH,
        )

    for b in bits:
        adapter_copy(0, b, 0).start()
    own_down.start()
    own_up.start()
    own_hidden.wait()

    def block_copy(d, right, j):
        return pltpu.make_async_remote_copy(
            src_ref=prod.at[d, j],
            dst_ref=recv.at[right, d, j],
            send_sem=z_send.at[d, j],
            recv_sem=z_recv.at[right, d, j],
            device_id={"mp": jnp.where(right == 1, (me + 1) % n, (me + n - 1) % n)},
            device_id_type=MESH,
        )

    def first_in_line(right):
        return jnp.where(right == 1, before, after) == 0

    def forward(item):
        d, right = visit(item // tiles)
        j = item % tiles

        @pl.when(jnp.logical_not(first_in_line(right)))
        def _():
            copy = block_copy(d, right, j)
            copy.wait_recv()
            prod[d, j] = (
                prod[d, j].astype(jnp.float32) + recv[right, d, j].astype(jnp.float32)
            ).astype(jnp.bfloat16)
            copy.start()

    queued = (n - 1) * tiles - 3 * tiles // 4
    start_forward = tiles + 1
    early = max(0, min(-(-(count - start_forward) // STRIDE), (n - 2) * tiles))

    @pl.loop(0, count)
    def _(t):
        slot = t % SLOTS

        @pl.when(t + SLOTS - 1 < count)
        def _():
            weight_copy(t + SLOTS - 1, (t + SLOTS - 1) % SLOTS).start()

        weight_copy(t, slot).wait()
        d, right = visit(t // tiles)
        j = t % tiles
        prod[d, j] = jnp.dot(
            hidden_ref[...], weights[slot], preferred_element_type=jnp.float32
        ).astype(jnp.bfloat16)

        @pl.when((t < queued) & first_in_line(right))
        def _():
            block_copy(d, right, j).start()

        if early:
            step = t - start_forward

            @pl.when((step >= 0) & (step % STRIDE == 0) & (step < early * STRIDE))
            def _():
                forward(jnp.maximum(step, 0) // STRIDE)

    @pl.loop(early, (n - 2) * tiles)
    def _(i):
        forward(i)

    def relay(i, before_last):
        held = [0]
        for b in bits:
            for s in held:
                if s:
                    adapter_copy(i, b, s).start()
            if b == bits[-1]:
                before_last()
            for s in held:
                adapter_copy(i, b, s).wait_recv()
            held = held + [s ^ b for s in held]

    def rest():
        for b in bits:
            adapter_copy(1, b, 0).start()

        @pl.loop((n - 2) * tiles, (n - 1) * tiles)
        def _(i):
            forward(i)

    relay(0, rest)
    own_down.wait()

    total_adapters = na * local_count
    stacked = store_down[...].reshape(total_adapters * rank, store_down.shape[2])
    every = lax.dot_general(
        stacked, hidden_ref[...], (((1,), (1,)), ((), ())), preferred_element_type=jnp.float32
    )
    ids = ids_ref[...].reshape(1, rows)
    part = jnp.zeros((rank, rows), jnp.float32)
    for g in range(total_adapters):
        part = part + jnp.where(ids == g, every[g * rank : (g + 1) * rank], 0.0)

    def factor_copy(right):
        return pltpu.make_async_remote_copy(
            src_ref=fac.at[right],
            dst_ref=fac_in.at[right],
            send_sem=f_send.at[right],
            recv_sem=f_recv.at[right],
            device_id={"mp": (me + 1) % n if right else (me + n - 1) % n},
            device_id_type=MESH,
        )

    mine = part.astype(jnp.bfloat16)
    fac[0] = mine
    fac[1] = mine
    ends = ((1, before, after), (0, after, before))
    for right, upstream, _ in ends:

        @pl.when(upstream == 0)
        def _(right=right):
            factor_copy(right).start()

    @pl.loop(queued, (n - 1) * tiles)
    def _(i):
        d, right = visit(i // tiles)

        @pl.when(first_in_line(right))
        def _():
            block_copy(d, right, i % tiles).start()

    relay(1, lambda: None)
    own_up.wait()
    fac_sum[...] = part
    for right, upstream, downstream, here in (
        (*ends[0], before < after), (*ends[1], before >= 0), (*ends[0], before >= after)
    ):

        @pl.when((upstream > 0) & here)
        def _(right=right, downstream=downstream):
            factor_copy(right).wait_recv()
            came = fac_in[right].astype(jnp.float32)
            fac_sum[...] += came

            @pl.when(downstream > 0)
            def _():
                fac[right] = (fac[right].astype(jnp.float32) + came).astype(jnp.bfloat16)
                factor_copy(right).start()

    factor = fac_sum[...]
    factor = (factor * inv_units).astype(jnp.bfloat16).astype(jnp.float32)
    for g in range(total_adapters):
        spread[g * rank : (g + 1) * rank, :] = jnp.where(ids == g, factor, 0.0).astype(
            jnp.bfloat16
        )
    turned = jnp.transpose(spread[...].astype(jnp.float32)).astype(jnp.bfloat16)
    for j in range(tiles):
        cols = slice(j * tile, (j + 1) * tile)
        lora[:, cols] = (
            jnp.dot(
                turned,
                store_up[:, :, cols].reshape(total_adapters * rank, tile),
                preferred_element_type=jnp.float32,
            )
            * out_scale
        ).astype(jnp.bfloat16)

    for s in range(local_count):
        g = plan_ref[s]
        mdown_ref[s] = store_down[g // local_count, pl.ds((g % local_count) * rank, rank), :]
        mup_ref[s] = store_up[g // local_count, pl.ds((g % local_count) * rank, rank), :]

    for j in range(tiles):
        cols = slice(j * tile, (j + 1) * tile)
        total[...] = prod[me, j].astype(jnp.float32)
        for right, there in ((1, before > 0), (0, after > 0)):

            @pl.when(there)
            def _(right=right, j=j):
                block_copy(me, jnp.int32(right), j).wait_recv()
                total[...] += recv[right, me, j].astype(jnp.float32)

        out_ref[:, cols] = (total[...] + lora[:, cols].astype(jnp.float32)).astype(jnp.bfloat16)

    @pl.loop(0, (n - 1) * tiles)
    def _(i):
        d, right = visit(i // tiles)
        block_copy(d, right, i % tiles).wait_send()

    for right, _, downstream in ends:

        @pl.when(downstream > 0)
        def _(right=right):
            factor_copy(right).wait_send()

    held = [0]
    for b in bits:
        for s in held:
            for i in range(2):
                adapter_copy(i, b, s).wait_send()
        held = held + [s ^ b for s in held]


def place(*refs):
    sources, targets, sems = refs[:3], refs[3:6], refs[6]
    copies = [pltpu.make_async_copy(a, b, sems.at[i]) for i, (a, b) in enumerate(zip(sources, targets))]
    for c in copies:
        c.start()
    for c in copies:
        c.wait()


def per_device(n, na, hidden, adapter_ids, down_weight, adapter_down, adapter_up, migration_plan):
    rows, units = hidden.shape
    local_count, rank, width = adapter_up.shape
    tile = min(256, width)
    tiles = width // tile
    stack = local_count * rank
    vmem = pl.BlockSpec(memory_space=pltpu.VMEM)
    anywhere = pl.BlockSpec(memory_space=pl.ANY)
    bf16 = jnp.bfloat16
    shapes = (
        jax.ShapeDtypeStruct((rows, width), bf16),
        jax.ShapeDtypeStruct(adapter_down.shape, bf16),
        jax.ShapeDtypeStruct(adapter_up.shape, bf16),
    )
    held = pl.pallas_call(
        functools.partial(
            kernel, n, na, tile, 1.0 / math.sqrt(units * n), 0.5 / math.sqrt(rank)
        ),
        out_shape=tuple(pltpu.VMEM(x.shape, x.dtype) for x in shapes),
        in_specs=[pl.BlockSpec(memory_space=pltpu.SMEM), vmem] + [anywhere] * 4,
        out_specs=(vmem, vmem, vmem),
        scratch_shapes=[
            pltpu.VMEM((SLOTS, units, tile), bf16),
            pltpu.VMEM((rows, units), bf16),
            pltpu.VMEM((n, tiles, rows, tile), bf16),
            pltpu.VMEM((2, n, tiles, rows, tile), bf16),
            pltpu.VMEM((na, stack, units), bf16),
            pltpu.VMEM((na, stack, width), bf16),
            pltpu.VMEM((2, rank, rows), bf16),
            pltpu.VMEM((2, rank, rows), bf16),
            pltpu.VMEM((rank, rows), jnp.float32),
            pltpu.VMEM((rows, width), bf16),
            pltpu.VMEM((na * stack, rows), bf16),
            pltpu.VMEM((rows, tile), jnp.float32),
            pltpu.SemaphoreType.DMA((SLOTS,)),
            pltpu.SemaphoreType.DMA((n, tiles)),
            pltpu.SemaphoreType.DMA((2, n, tiles)),
            pltpu.SemaphoreType.DMA((3,)),
            pltpu.SemaphoreType.DMA((2, na)),
            pltpu.SemaphoreType.DMA((2, na)),
            pltpu.SemaphoreType.DMA((2,)),
            pltpu.SemaphoreType.DMA((2,)),
        ],
        compiler_params=pltpu.CompilerParams(
            collective_id=0, has_side_effects=True, vmem_limit_bytes=56 << 20
        ),
    )(
        migration_plan,
        adapter_ids,
        hidden,
        adapter_down.reshape(stack, units),
        adapter_up.reshape(stack, width),
        down_weight,
    )
    return pl.pallas_call(
        place,
        out_shape=shapes,
        in_specs=[vmem] * 3,
        out_specs=(anywhere,) * 3,
        scratch_shapes=[pltpu.SemaphoreType.DMA((3,))],
    )(*(pltpu.with_memory_space_constraint(x, pltpu.VMEM) for x in held))


def solution(mesh):
    placed = (
        P(("groups", "adapter"), "mp"),
        P(("groups", "adapter")),
        P("mp", None),
        P(("groups", "adapter"), None, "mp"),
        P(("groups", "adapter"), None, "mp"),
        P(("groups", "adapter")),
    )
    return jax.shard_map(
        functools.partial(per_device, mesh.shape["mp"], mesh.shape["adapter"]),
        mesh=mesh,
        in_specs=placed,
        out_specs=(
            P(("groups", "adapter"), "mp"),
            P(("groups", "adapter"), None, "mp"),
            P(("groups", "adapter"), None, "mp"),
        ),
        check_vma=False,
    )
```
